32 devices in a mesh: groups: 2 (over x), src: 8 (over z, y), rcv: 2 (over core).
Axes of the slice: x: 2, y: 2, z: 4, core: 2. Of those that a mesh axis runs over, the one named last changes fastest.
Arguments:
- spectra: bfloat16 [1280, 2, 2, 4096], P(('groups', 'src'), None, None, 'rcv'), parts along dimension 0, may hold values from -6 to 6
- pair_bins: int32 [1280, 80], P(('groups', 'src')), parts along dimension 0, may hold values from 0 to 15
- owners: int32 [32], P('groups'), parts along dimension 0, may hold values from 0 to 15, as said below
Outputs:
- bin_stacks: float32 [64, 2, 4096], P(('groups', 'src', 'rcv')), parts along dimension 0
The draws below stay inside these ranges and needn't reach their ends.
There are 2 independent parts, one for each index of `groups`. The reference program is written for one: setup_inputs(seed, part) draws one part's arguments, and reference() takes and returns one part's arrays. A program takes and returns all parts, laid end to end along the dimension named above; each array names one. Nothing has to cross between parts.
Inputs may be any that keep to these rules, and one draw needn't show every extreme that they name: `owners`: each device owns at most 2 bins and some device owns exactly 2.
All inputs are finite; a program needn't handle non-finite values.
Results may differ from the reference program's by a relative error of at most 0.004.
Values may be sent and summed in bfloat16 or wider, within the bound.
A program may use at most 64 MiB of HBM per device.

```python
import jax
import jax.numpy as jnp
from jax import lax

CB = 80
W = 2
F = 4096
HALF = 32
CH = 640
NB = 16
ND = 16
CAP = 2
N_SRC = 8


def draw_owners(key, part):
    first_key, second_key = jax.random.split(jax.random.fold_in(key, 7))
    order = jax.random.permutation(first_key, ND * CAP)
    owner_slot = order // CAP
    leader = owner_slot[0]
    priority = jnp.where(owner_slot == leader, -1, jnp.arange(ND * CAP))
    ranked = jnp.argsort(priority, stable=True)
    chosen = owner_slot[ranked[:NB]]
    shuffle = jax.random.permutation(second_key, NB)
    return chosen[shuffle].astype(jnp.int32)


def with_ends(result, stream_key, low, high):
    longest = result.shape.index(max(result.shape))
    spots = []
    for shift in (0, 1):
        where = [jax.random.randint(jax.random.fold_in(stream_key, axis), (), 0, length) for axis, length in enumerate(result.shape)]
        where[longest] = (where[longest] + shift) % result.shape[longest]
        spots.append(tuple(where))
    return result.at[spots[0]].set(low).at[spots[1]].set(high)


def level_of(own_key, shape, pieces, smallest, high):
    loudness, own = 1.0, jax.random.fold_in(own_key, 6)
    for axis_at, blocks in pieces:
        draws = jnp.exp(jax.random.uniform(jax.random.fold_in(own, axis_at), (blocks,), jnp.float32, smallest / len(pieces), high / len(pieces)))
        loudness = loudness * jnp.repeat(draws, shape[axis_at] // blocks).reshape([-1 if axis == axis_at else 1 for axis in range(len(shape))])
    return loudness


def centred(own_key, dims, spread, reach, shards=(), kind=jnp.bfloat16):
    entries = jax.random.normal(own_key, dims, jnp.float32) * spread
    if len(shards) > 0:
        entries = level_of(own_key, dims, shards, -0.22, 0.18) * entries
    return jnp.clip(entries, min=-reach, max=reach).astype(kind)


def setup_inputs(seed: int = 0, part: int = 0) -> dict:
    seeds = jax.random.split(jax.random.key(seed), 4)
    part_splits = jax.random.split(jax.random.fold_in(seeds[3], part), 4)
    return {
        "spectra": centred(part_splits[0], (CH, W, 2, F), 1.0, 6.0, ((0, 8), (3, 2))),
        "pair_bins": with_ends(jax.random.randint(part_splits[1], (CH, CB), 0, NB), jax.random.fold_in(part_splits[1], 1), 0, NB - 1).astype(jnp.int32),
        "owners": draw_owners(jax.random.fold_in(jax.random.fold_in(seeds[3], part), 71), part),
    }


smooth_eps = 1e-06

def whiten(spectra):
    values = spectra.astype(jnp.float32)
    magnitude = jnp.sqrt(values[:, :, 0] ** 2 + values[:, :, 1] ** 2)
    padded = jnp.pad(magnitude, ((0, 0), (0, 0), (HALF, HALF)))
    total = jnp.zeros_like(magnitude)
    for offset in range(2 * HALF + 1):
        total = total + padded[:, :, offset:offset + F]
    smooth = total / (2 * HALF + 1)
    return (values / (smooth[:, :, None, :] + smooth_eps)).astype(jnp.bfloat16)

def reference(spectra, pair_bins, owners):
    white_half = whiten(spectra)
    white = lax.optimization_barrier(white_half).astype(jnp.float32)
    padded = jnp.concatenate([white, jnp.zeros((CB, W, 2, F), jnp.float32)], axis=0)
    channel_ids = jnp.arange(CH, dtype=jnp.int32)

    def per_source(carry, inputs):
        source, bins_row, channel = inputs
        block_id = channel // CB
        start = ((block_id + 1) * CB).astype(jnp.int32)
        receivers = lax.dynamic_slice_in_dim(padded, start, CB, 0)
        valid = (block_id + 1 < N_SRC).astype(jnp.float32)
        src_re = source[:, 0]
        src_im = source[:, 1]
        corr_re = lax.optimization_barrier(jnp.sum(src_re[None] * receivers[:, :, 0] + src_im[None] * receivers[:, :, 1], axis=1))
        corr_im = lax.optimization_barrier(jnp.sum(src_im[None] * receivers[:, :, 0] - src_re[None] * receivers[:, :, 1], axis=1))
        stacked = jnp.stack([corr_re, corr_im], axis=1) * valid
        stack_sum = carry[0] + jax.ops.segment_sum(stacked, bins_row, num_segments=NB)
        count_sum = carry[1] + jax.ops.segment_sum(jnp.ones((CB,), jnp.float32) * valid, bins_row, num_segments=NB)
        return ((stack_sum, count_sum), None)
    init = (jnp.zeros((NB, 2, F), jnp.float32), jnp.zeros((NB,), jnp.float32))
    (stack, counts), _ = lax.scan(per_source, init, (white, pair_bins, channel_ids))
    same = owners[:, None] == owners[None, :]
    earlier = jnp.arange(NB, dtype=jnp.int32)[None, :] < jnp.arange(NB, dtype=jnp.int32)[:, None]
    slot = lax.optimization_barrier(jnp.sum((same & earlier).astype(jnp.int32), axis=1))
    rows = (owners * CAP + slot).astype(jnp.int32)
    scaled = stack / jnp.sqrt(jnp.maximum(counts, 1.0))[:, None, None]
    return jnp.zeros((ND * CAP, 2, F), jnp.float32).at[rows].set(scaled)
```

```python
import functools

import jax
import jax.numpy as jnp
from jax import lax
from jax.experimental import pallas as pl
from jax.experimental.pallas import tpu as pltpu
from jax.sharding import PartitionSpec as P

HALF = 32
CAP = 2
EDGE = 128
CHUNK = 256
smooth_eps = 1e-06
MESH = pl.DeviceIdType.MESH


def kernel(
    dims,
    x_ref,
    lab_ref,
    labt_ref,
    rows_ref,
    tiled_ref,
    out_ref,
    white,
    near,
    far,
    halo,
    mag_hi,
    mag_lo,
    band,
    onehot,
    own,
    prod,
    acc,
    send_part,
    recv_part,
    lab_in,
    count_out,
    count_in,
    near_send,
    near_recv,
    far_send,
    far_recv,
    halo_sems,
    lab_sems,
    count_send,
    count_recv,
    part_send,
    part_recv,
):
    nsrc, nrcv, nbins, local, windows, chunks, group = dims
    half = chunks // 2
    width = chunks * CHUNK
    ndev = nsrc * nrcv
    s = lax.axis_index("src")
    r = lax.axis_index("rcv")
    me = s * nrcv + r
    par = lax.rem(s, 2)
    f32 = jnp.float32

    barrier = pltpu.get_barrier_semaphore()

    def greet(k, carry):
        o = lax.rem(me + k, ndev)
        pl.semaphore_signal(
            barrier,
            inc=1,
            device_id={"src": o // nrcv, "rcv": lax.rem(o, nrcv)},
            device_id_type=MESH,
        )
        return carry

    lax.fori_loop(1, ndev, greet, 0)

    def place(h, t):
        return h * half + r * (half - 1) + t * (1 - 2 * r)

    def put_magnitude(re, im, row, at, size):
        re = re.astype(f32)
        im = im.astype(f32)
        m = jnp.sqrt(re * re + im * im)
        hi = m.astype(jnp.bfloat16)
        mag_hi[pl.ds(row, local), pl.ds(at, size)] = hi
        mag_lo[pl.ds(row, local), pl.ds(at, size)] = (m - hi.astype(f32)).astype(jnp.bfloat16)

    zero = jnp.zeros((windows * local, EDGE), jnp.bfloat16)
    for buffer in (mag_hi, mag_lo):
        buffer[:, :EDGE] = zero
        buffer[:, EDGE + width :] = zero

    def magnitudes(j, carry):
        for w in range(windows):
            put_magnitude(
                x_ref[j, 2 * w],
                x_ref[j, 2 * w + 1],
                w * local,
                pl.multiple_of(EDGE + j * CHUNK, 128),
                CHUNK,
            )
        return carry

    lax.fori_loop(0, chunks, magnitudes, 0)
    tall = CHUNK + 2 * EDGE
    k_ids = lax.broadcasted_iota(jnp.int32, (tall, CHUNK), 0) - EDGE
    n_ids = lax.broadcasted_iota(jnp.int32, (tall, CHUNK), 1)
    band[...] = jnp.where((k_ids >= n_ids - HALF) & (k_ids <= n_ids + HALF), 1.0, 0.0).astype(
        jnp.bfloat16
    )

    def whiten(j):
        span = pl.ds(pl.multiple_of(j * CHUNK, 128), tall)
        total = jnp.dot(mag_hi[:, span], band[...], preferred_element_type=f32)
        total = total + jnp.dot(mag_lo[:, span], band[...], preferred_element_type=f32)
        inverse = 1.0 / (total / (2 * HALF + 1) + smooth_eps)
        for w in range(windows):
            part = inverse[w * local : (w + 1) * local]
            for p in range(2):
                white[j, 2 * w + p] = (x_ref[j, 2 * w + p].astype(f32) * part).astype(jnp.bfloat16)

    partner = s + 1 - 2 * par
    beyond = s + 2 - 4 * par
    sends_far = (beyond >= 0) & (beyond < nsrc)
    back = s - 2 + 4 * par
    has_far = (back >= 0) & (back < nsrc)

    def near_copy(t):
        return pltpu.make_async_remote_copy(
            src_ref=white.at[place(1 - par, t)],
            dst_ref=near.at[t],
            send_sem=near_send.at[t],
            recv_sem=near_recv.at[t],
            device_id={"src": partner},
            device_id_type=MESH,
        )

    def far_copy(t):
        return pltpu.make_async_remote_copy(
            src_ref=near.at[t],
            dst_ref=far.at[t],
            send_sem=far_send.at[t],
            recv_sem=far_recv.at[t],
            device_id={"src": beyond},
            device_id_type=MESH,
        )

    halo_copy = pltpu.make_async_remote_copy(
        src_ref=x_ref.at[
            (1 - r) * (chunks - 1), :, :, pl.ds(pl.multiple_of((1 - r) * (CHUNK - EDGE), 128), EDGE)
        ],
        dst_ref=halo,
        send_sem=halo_sems.at[0],
        recv_sem=halo_sems.at[1],
        device_id={"rcv": 1 - r},
        device_id_type=MESH,
    )
    lab_copy = pltpu.make_async_remote_copy(
        src_ref=labt_ref,
        dst_ref=lab_in,
        send_sem=lab_sems.at[0],
        recv_sem=lab_sems.at[1],
        device_id={"src": s + 1},
        device_id_type=MESH,
    )

    whiten(place(1 - par, 0))
    pl.semaphore_wait(barrier, ndev - 1)
    halo_copy.start()
    near_copy(0).start()

    @pl.when(s + 1 < nsrc)
    def _():
        lab_copy.start()

    def send_next(t, carry):
        whiten(place(1 - par, t))
        near_copy(t).start()
        return carry

    lax.fori_loop(1, half - 1, send_next, 0)
    halo_copy.wait_recv()
    for w in range(windows):
        put_magnitude(
            halo[2 * w],
            halo[2 * w + 1],
            w * local,
            pl.multiple_of((1 - r) * (EDGE + width), 128),
            EDGE,
        )
    whiten(place(1 - par, half - 1))
    near_copy(half - 1).start()

    labels = lab_ref[...]
    lanes = count_out.shape[1]
    lane_ids = lax.broadcasted_iota(jnp.int32, (8, lanes), 1)
    valid = (s + 1 < nsrc).astype(f32)

    def expand(b, counted):
        hits = jnp.where(labels == b, 1.0, 0.0).astype(f32)
        onehot[0, pl.ds(pl.multiple_of(b * local, 16), local), :] = hits.astype(jnp.bfloat16)
        found = jnp.sum(jnp.sum(hits, axis=0, keepdims=True), axis=1, keepdims=True)
        return counted + jnp.where(lane_ids == b, found, 0.0)

    counted = lax.fori_loop(0, nbins, expand, jnp.zeros((8, lanes), f32)) * valid
    count_out[...] = counted
    count_in[s] = counted

    def count_copy(o, slot):
        return pltpu.make_async_remote_copy(
            src_ref=count_out,
            dst_ref=count_in.at[slot],
            send_sem=count_send.at[o],
            recv_sem=count_recv.at[slot],
            device_id={"src": o},
            device_id_type=MESH,
        )

    def send_count(k, carry):
        count_copy(lax.rem(s + k, nsrc), s).start()
        return carry

    lax.fori_loop(1, nsrc, send_count, 0)

    def keep(t, carry):
        whiten(place(par, t))
        return carry

    lax.fori_loop(0, half, keep, 0)

    @pl.when(s > 0)
    def _():
        lab_copy.wait_recv()
        previous = lab_in[...]

        def expand_previous(b, carry):
            onehot[1, pl.ds(pl.multiple_of(b * local, 16), local), :] = jnp.where(
                previous == b, 1.0, 0.0
            ).astype(jnp.bfloat16)
            return carry

        lax.fori_loop(0, nbins, expand_previous, 0)

    def correlate(which, other, t, first):
        for k in range(2 * windows):
            own[k] = white[place(par, t), k].astype(f32)
        sign = (1 - 2 * which).astype(f32)
        rows = group * local

        def some(g, carry):
            picked = onehot[which, pl.ds(pl.multiple_of(g * rows, 16), rows), :]
            for k in range(2 * windows):
                prod[k] = jnp.dot(picked, other[t, k], preferred_element_type=f32)
            res, ims = [], []
            for b in range(group):
                at = slice(b * local, (b + 1) * local)
                re = jnp.zeros((local, CHUNK), f32)
                im = jnp.zeros((local, CHUNK), f32)
                for w in range(windows):
                    p_re, p_im = prod[2 * w, at], prod[2 * w + 1, at]
                    o_re, o_im = own[2 * w], own[2 * w + 1]
                    re = re + (o_re * p_re + o_im * p_im)
                    im = im + (o_im * p_re - o_re * p_im)
                res.append(jnp.sum(re, axis=0, keepdims=True))
                ims.append(jnp.sum(im, axis=0, keepdims=True))
            at = pl.ds(pl.multiple_of(g * group, group), group)
            re = jnp.concatenate(res, axis=0)
            im = jnp.concatenate(ims, axis=0) * sign
            if first:
                acc[t, 0, at] = re
                acc[t, 1, at] = im
            else:
                acc[t, 0, at] += re
                acc[t, 1, at] += im
            return carry

        lax.fori_loop(0, nbins // group, some, 0)

    def near_turn(t, carry):
        near_copy(t).wait_recv()

        @pl.when(sends_far)
        def _():
            far_copy(t).start()

        correlate(par, near, t, True)
        return carry

    def far_turn(t, carry):
        far_copy(t).wait_recv()
        correlate(1 - par, far, t, False)
        return carry

    def turn(t, carry):
        near_turn(t, 0)

        @pl.when((t > 0) & has_far)
        def _():
            far_turn(t - 1, 0)

        return carry

    lax.fori_loop(0, half, turn, 0)

    @pl.when(has_far)
    def _():
        far_turn(half - 1, 0)

    lines = CAP * 2 * half
    cols = half * 2 * nbins
    stacked = acc[...].reshape(cols, CHUNK).astype(jnp.bfloat16)
    batch = 16
    row_ids = lax.broadcasted_iota(jnp.int32, (batch * lines, cols), 0)
    col_ids = lax.broadcasted_iota(jnp.int32, (batch * lines, cols), 1)
    row_line = lax.rem(row_ids, 2 * half)
    col_turn = col_ids // (2 * nbins)
    col_line = lax.rem(col_ids // nbins, 2) * half + r * (half - 1) + col_turn * (1 - 2 * r)
    same_line = row_line == col_line
    row_slot = row_ids // (2 * half)

    def route(g, carry):
        pick = same_line & (tiled_ref[...] == row_slot + g * (batch * CAP))
        at = pl.ds(pl.multiple_of(g * (batch * lines), 16), batch * lines)
        pick = jnp.where(pick, 1.0, 0.0).astype(jnp.bfloat16)
        send_part[at] = jnp.dot(pick, stacked, preferred_element_type=f32).astype(jnp.bfloat16)
        return carry

    lax.fori_loop(0, ndev // batch, route, 0)

    def part_copy(o, slot):
        return pltpu.make_async_remote_copy(
            src_ref=send_part.at[pl.ds(pl.multiple_of(o * lines, 16), lines)],
            dst_ref=recv_part.at[slot],
            send_sem=part_send.at[o],
            recv_sem=part_recv.at[slot],
            device_id={"src": o // nrcv, "rcv": lax.rem(o, nrcv)},
            device_id_type=MESH,
        )

    def send_one(k, carry):
        part_copy(lax.rem(me + k, ndev), me).start()
        return carry

    lax.fori_loop(1, ndev, send_one, 0)
    recv_part[me] = send_part[pl.ds(pl.multiple_of(me * lines, 16), lines)]

    def take_count(k, carry):
        o = lax.rem(s + k, nsrc)
        count_copy(o, o).wait_recv()
        return carry

    lax.fori_loop(1, nsrc, take_count, 0)
    counts = jnp.sum(count_in[...], axis=0)[0:1]
    mine = [
        jnp.sum(jnp.where(rows_ref[...] == me * CAP + c, counts, 0.0), axis=1, keepdims=True)
        for c in range(CAP)
    ]
    line_ids = lax.broadcasted_iota(jnp.int32, (lines, 1), 0) // (2 * half)
    norm = jnp.zeros((lines, 1), f32)
    for c in range(CAP):
        norm = jnp.where(line_ids == c, jnp.sqrt(jnp.maximum(mine[c], 1.0)), norm)

    def take_part(k, carry):
        o = lax.rem(me + k, ndev)
        part_copy(o, o).wait_recv()
        return carry

    lax.fori_loop(1, ndev, take_part, 0)
    for rr in range(nrcv):
        for pp in range(2):

            def add(z, total):
                return total + recv_part[(2 * z + pp) * nrcv + rr].astype(f32)

            total = lax.fori_loop(0, nsrc // 2, add, jnp.zeros((lines, CHUNK), f32))
            out_ref[rr * 2 + pp] = total / norm

    for t in range(half):
        near_copy(t).wait_send()

    @pl.when(sends_far)
    def _():
        for t in range(half):
            far_copy(t).wait_send()

    halo_copy.wait_send()

    @pl.when(s + 1 < nsrc)
    def _():
        lab_copy.wait_send()

    def end_count(k, carry):
        count_copy(lax.rem(s + k, nsrc), s).wait_send()
        return carry

    lax.fori_loop(1, nsrc, end_count, 0)

    def end_part(k, carry):
        part_copy(lax.rem(me + k, ndev), me).wait_send()
        return carry

    lax.fori_loop(1, ndev, end_part, 0)


def per_device(spectra, pair_bins, owners):
    local, windows, _, width = spectra.shape
    nbins = owners.shape[0]
    nsrc = lax.axis_size("src")
    nrcv = lax.axis_size("rcv")
    ndev = nsrc * nrcv
    chunks = width // CHUNK
    half = chunks // 2
    lines = CAP * 2 * half
    lanes = -(-nbins // 128) * 128
    group = 8
    x = spectra.reshape(local, windows * 2, chunks, CHUNK).transpose(2, 1, 0, 3)
    bin_ids = jnp.arange(nbins, dtype=jnp.int32)
    same = owners[:, None] == owners[None, :]
    earlier = bin_ids[None, :] < bin_ids[:, None]
    rows = owners * CAP + jnp.sum((same & earlier).astype(jnp.int32), axis=1)
    rows_row = jnp.pad(rows, (0, lanes - nbins), constant_values=-1)[None]
    tiled = jnp.tile(rows, 2 * half)[None]
    dims = (nsrc, nrcv, nbins, local, windows, chunks, group)
    bf16, f32 = jnp.bfloat16, jnp.float32
    dma = pltpu.SemaphoreType.DMA
    vmem = pl.BlockSpec(memory_space=pltpu.VMEM)
    out = pl.pallas_call(
        functools.partial(kernel, dims),
        out_shape=jax.ShapeDtypeStruct((2 * nrcv, lines, CHUNK), f32),
        in_specs=[vmem] * 5,
        out_specs=vmem,
        scratch_shapes=[
            pltpu.VMEM((chunks, 2 * windows, local, CHUNK), bf16),
            pltpu.VMEM((half, 2 * windows, local, CHUNK), bf16),
            pltpu.VMEM((half, 2 * windows, local, CHUNK), bf16),
            pltpu.VMEM((2 * windows, local, EDGE), bf16),
            pltpu.VMEM((windows * local, width + 2 * EDGE), bf16),
            pltpu.VMEM((windows * local, width + 2 * EDGE), bf16),
            pltpu.VMEM((CHUNK + 2 * EDGE, CHUNK), bf16),
            pltpu.VMEM((2, nbins * local, local), bf16),
            pltpu.VMEM((2 * windows, local, CHUNK), f32),
            pltpu.VMEM((2 * windows, group * local, CHUNK), f32),
            pltpu.VMEM((half, 2, nbins, CHUNK), f32),
            pltpu.VMEM((ndev * lines, CHUNK), bf16),
            pltpu.VMEM((ndev, lines, CHUNK), bf16),
            pltpu.VMEM((local, local), jnp.int32),
            pltpu.VMEM((8, lanes), f32),
            pltpu.VMEM((nsrc, 8, lanes), f32),
            dma((half,)),
            dma((half,)),
            dma((half,)),
            dma((half,)),
            dma((2,)),
            dma((2,)),
            dma((nsrc,)),
            dma((nsrc,)),
            dma((ndev,)),
            dma((ndev,)),
        ],
        compiler_params=pltpu.CompilerParams(
            collective_id=0, has_side_effects=True, vmem_limit_bytes=48 * 1024 * 1024
        ),
    )(x, pair_bins, pair_bins.T, rows_row, tiled)
    out = out.reshape(nrcv * 2, CAP, 2, half, CHUNK).transpose(1, 2, 0, 3, 4)
    return out.reshape(CAP, 2, nrcv * width)


def solution(mesh):
    in_specs = (P(("groups", "src"), None, None, "rcv"), P(("groups", "src"), None), P("groups"))
    out_specs = P(("groups", "src", "rcv"), None, None)
    return jax.shard_map(
        per_device, mesh=mesh, in_specs=in_specs, out_specs=out_specs, check_vma=False
    )
```

```python
import functools

import jax
import jax.numpy as jnp
from jax import lax
from jax.experimental import pallas as pl
from jax.experimental.pallas import tpu as pltpu
from jax.sharding import PartitionSpec as P

HALF = 32
CAP = 2
EDGE = 128
CHUNK = 256
smooth_eps = 1e-06
MESH = pl.DeviceIdType.MESH


def kernel(
    dims,
    x_ref,
    lab_ref,
    labt_ref,
    rows_ref,
    tiled_ref,
    out_ref,
    white,
    near,
    far,
    halo,
    mag_hi,
    mag_lo,
    band,
    onehot,
    own,
    prod,
    acc,
    pick,
    send_part,
    recv_part,
    lab_in,
    count_out,
    count_in,
    near_send,
    near_recv,
    far_send,
    far_recv,
    halo_sems,
    lab_sems,
    count_send,
    count_recv,
    part_send,
    part_recv,
):
    nsrc, nrcv, nbins, local, windows, chunks, group = dims
    half = chunks // 2
    width = chunks * CHUNK
    ndev = nsrc * nrcv
    s = lax.axis_index("src")
    r = lax.axis_index("rcv")
    me = s * nrcv + r
    par = lax.rem(s, 2)
    f32 = jnp.float32

    barrier = pltpu.get_barrier_semaphore()

    def greet(k, carry):
        o = lax.rem(me + k, ndev)
        pl.semaphore_signal(
            barrier,
            inc=1,
            device_id={"src": o // nrcv, "rcv": lax.rem(o, nrcv)},
            device_id_type=MESH,
        )
        return carry

    lax.fori_loop(1, ndev, greet, 0)

    def place(h, t):
        return h * half + r * (half - 1) + t * (1 - 2 * r)

    def put_magnitude(re, im, row, at, size):
        re = re.astype(f32)
        im = im.astype(f32)
        m = jnp.sqrt(re * re + im * im)
        hi = m.astype(jnp.bfloat16)
        mag_hi[pl.ds(row, local), pl.ds(at, size)] = hi
        mag_lo[pl.ds(row, local), pl.ds(at, size)] = (m - hi.astype(f32)).astype(jnp.bfloat16)

    zero = jnp.zeros((windows * local, EDGE), jnp.bfloat16)
    for buffer in (mag_hi, mag_lo):
        buffer[:, :EDGE] = zero
        buffer[:, EDGE + width :] = zero

    def magnitudes(j, carry):
        at = pl.ds(pl.multiple_of(j * CHUNK, 128), CHUNK)
        for w in range(windows):
            put_magnitude(
                x_ref[2 * w, :, at],
                x_ref[2 * w + 1, :, at],
                w * local,
                pl.multiple_of(EDGE + j * CHUNK, 128),
                CHUNK,
            )
        return carry

    def inside(j):
        return jnp.minimum(jnp.maximum(j, 0), chunks - 1)

    for t in range(-1, 2):
        magnitudes(inside(place(1 - par, t)), 0)
    tall = CHUNK + 2 * EDGE
    k_ids = lax.broadcasted_iota(jnp.int32, (tall, CHUNK), 0) - EDGE
    n_ids = lax.broadcasted_iota(jnp.int32, (tall, CHUNK), 1)
    band[...] = jnp.where((k_ids >= n_ids - HALF) & (k_ids <= n_ids + HALF), 1.0, 0.0).astype(
        jnp.bfloat16
    )

    def whiten(j):
        span = pl.ds(pl.multiple_of(j * CHUNK, 128), tall)
        total = jnp.dot(mag_hi[:, span], band[...], preferred_element_type=f32)
        total = total + jnp.dot(mag_lo[:, span], band[...], preferred_element_type=f32)
        inverse = 1.0 / (total / (2 * HALF + 1) + smooth_eps)
        for w in range(windows):
            part = inverse[w * local : (w + 1) * local]
            for p in range(2):
                raw = x_ref[2 * w + p, :, pl.ds(pl.multiple_of(j * CHUNK, 128), CHUNK)]
                white[j, 2 * w + p] = (raw.astype(f32) * part).astype(jnp.bfloat16)

    partner = s + 1 - 2 * par
    beyond = s + 2 - 4 * par
    sends_far = (beyond >= 0) & (beyond < nsrc)
    back = s - 2 + 4 * par
    has_far = (back >= 0) & (back < nsrc)

    def near_copy(t, k):
        return pltpu.make_async_remote_copy(
            src_ref=white.at[place(1 - par, t), k],
            dst_ref=near.at[t, k],
            send_sem=near_send.at[t, k],
            recv_sem=near_recv.at[t, k],
            device_id={"src": partner},
            device_id_type=MESH,
        )

    def far_copy(t, k):
        return pltpu.make_async_remote_copy(
            src_ref=near.at[t, k],
            dst_ref=far.at[t, k],
            send_sem=far_send.at[t, k],
            recv_sem=far_recv.at[t, k],
            device_id={"src": beyond},
            device_id_type=MESH,
        )

    halo_copy = pltpu.make_async_remote_copy(
        src_ref=x_ref.at[
            :, :, pl.ds(pl.multiple_of((1 - r) * (width - EDGE), 128), EDGE)
        ],
        dst_ref=halo,
        send_sem=halo_sems.at[0],
        recv_sem=halo_sems.at[1],
        device_id={"rcv": 1 - r},
        device_id_type=MESH,
    )
    lab_copy = pltpu.make_async_remote_copy(
        src_ref=labt_ref,
        dst_ref=lab_in,
        send_sem=lab_sems.at[0],
        recv_sem=lab_sems.at[1],
        device_id={"src": s + 1},
        device_id_type=MESH,
    )

    whiten(place(1 - par, 0))
    pl.semaphore_wait(barrier, ndev - 1)
    halo_copy.start()

    def send_near(t):
        for k in range(2 * windows):
            near_copy(t, k).start()

    send_near(0)

    @pl.when(s + 1 < nsrc)
    def _():
        lab_copy.start()

    def send_next(t, carry):
        magnitudes(inside(place(1 - par, t + 1)), 0)
        whiten(place(1 - par, t))
        send_near(t)
        return carry

    lax.fori_loop(1, half - 1, send_next, 0)
    magnitudes(inside(place(1 - par, half)), 0)
    halo_copy.wait_recv()
    for w in range(windows):
        put_magnitude(
            halo[2 * w],
            halo[2 * w + 1],
            w * local,
            pl.multiple_of((1 - r) * (EDGE + width), 128),
            EDGE,
        )
    whiten(place(1 - par, half - 1))
    send_near(half - 1)

    labels = lab_ref[...]
    lanes = count_out.shape[1]
    lane_ids = lax.broadcasted_iota(jnp.int32, (8, lanes), 1)
    valid = (s + 1 < nsrc).astype(f32)

    def expand(b, counted):
        hits = jnp.where(labels == b, 1.0, 0.0).astype(f32)
        onehot[0, pl.ds(pl.multiple_of(b * local, 16), local), :] = hits.astype(jnp.bfloat16)
        found = jnp.sum(jnp.sum(hits, axis=0, keepdims=True), axis=1, keepdims=True)
        return counted + jnp.where(lane_ids == b, found, 0.0)

    counted = lax.fori_loop(0, nbins, expand, jnp.zeros((8, lanes), f32)) * valid
    count_out[...] = counted
    count_in[s] = counted

    def count_copy(o, slot):
        return pltpu.make_async_remote_copy(
            src_ref=count_out,
            dst_ref=count_in.at[slot],
            send_sem=count_send.at[o],
            recv_sem=count_recv.at[slot],
            device_id={"src": o},
            device_id_type=MESH,
        )

    def send_count(k, carry):
        count_copy(lax.rem(s + k, nsrc), s).start()
        return carry

    lax.fori_loop(1, nsrc, send_count, 0)

    def keep_magnitude(t, carry):
        return magnitudes(place(par, t), carry)

    lax.fori_loop(0, half, keep_magnitude, 0)

    def keep(t, carry):
        whiten(place(par, t))
        return carry

    lax.fori_loop(0, half, keep, 0)

    @pl.when(s > 0)
    def _():
        lab_copy.wait_recv()
        previous = lab_in[...]

        def expand_previous(b, carry):
            onehot[1, pl.ds(pl.multiple_of(b * local, 16), local), :] = jnp.where(
                previous == b, 1.0, 0.0
            ).astype(jnp.bfloat16)
            return carry

        lax.fori_loop(0, nbins, expand_previous, 0)

    lines = CAP * 2 * half
    cols = half * 2 * nbins
    batch = 16
    row_ids = lax.broadcasted_iota(jnp.int32, (batch * lines, cols), 0)
    col_ids = lax.broadcasted_iota(jnp.int32, (batch * lines, cols), 1)
    row_line = lax.rem(row_ids, 2 * half)
    col_turn = col_ids // (2 * nbins)
    col_line = lax.rem(col_ids // nbins, 2) * half + r * (half - 1) + col_turn * (1 - 2 * r)
    same_line = row_line == col_line
    row_slot = row_ids // (2 * half)

    def prepare(g, carry):
        chosen = same_line & (tiled_ref[...] == row_slot + g * (batch * CAP))
        at = pl.ds(pl.multiple_of(g * (batch * lines), 16), batch * lines)
        pick[at] = jnp.where(chosen, 1.0, 0.0).astype(jnp.bfloat16)
        return carry

    lax.fori_loop(0, ndev // batch, prepare, 0)

    def correlate(which, other, t, first):
        for k in range(2 * windows):
            own[k] = white[place(par, t), k].astype(f32)
        sign = (1 - 2 * which).astype(f32)
        rows = group * local

        def some(g, carry):
            picked = onehot[which, pl.ds(pl.multiple_of(g * rows, 16), rows), :]
            for k in range(2 * windows):
                prod[k] = jnp.dot(picked, other[t, k], preferred_element_type=f32)
            res, ims = [], []
            for b in range(group):
                at = slice(b * local, (b + 1) * local)
                re = jnp.zeros((local, CHUNK), f32)
                im = jnp.zeros((local, CHUNK), f32)
                for w in range(windows):
                    p_re, p_im = prod[2 * w, at], prod[2 * w + 1, at]
                    o_re, o_im = own[2 * w], own[2 * w + 1]
                    re = re + (o_re * p_re + o_im * p_im)
                    im = im + (o_im * p_re - o_re * p_im)
                res.append(jnp.sum(re, axis=0, keepdims=True))
                ims.append(jnp.sum(im, axis=0, keepdims=True))
            at = pl.ds(pl.multiple_of(g * group, group), group)
            re = jnp.concatenate(res, axis=0)
            im = jnp.concatenate(ims, axis=0) * sign
            if first:
                acc[t, 0, at] = re
                acc[t, 1, at] = im
            else:
                acc[t, 0, at] += re
                acc[t, 1, at] += im
            return carry

        lax.fori_loop(0, nbins // group, some, 0)

    def near_turn(t, carry):
        for k in range(2 * windows):
            near_copy(t, k).wait_recv()

            @pl.when(sends_far)
            def _():
                far_copy(t, k).start()

        correlate(par, near, t, True)
        return carry

    def far_turn(t, carry):
        for k in range(2 * windows):
            far_copy(t, k).wait_recv()
        correlate(1 - par, far, t, False)
        return carry

    def turn(t, carry):
        near_turn(t, 0)

        @pl.when((t > 0) & has_far)
        def _():
            far_turn(t - 1, 0)

        return carry

    lax.fori_loop(0, half, turn, 0)

    def take_count(k, carry):
        o = lax.rem(s + k, nsrc)
        count_copy(o, o).wait_recv()
        return carry

    lax.fori_loop(1, nsrc, take_count, 0)
    counts = jnp.sum(count_in[...], axis=0)[0:1]
    mine = [
        jnp.sum(jnp.where(rows_ref[...] == me * CAP + c, counts, 0.0), axis=1, keepdims=True)
        for c in range(CAP)
    ]
    line_ids = lax.broadcasted_iota(jnp.int32, (lines, 1), 0) // (2 * half)
    norm = jnp.zeros((lines, 1), f32)
    for c in range(CAP):
        norm = jnp.where(line_ids == c, jnp.sqrt(jnp.maximum(mine[c], 1.0)), norm)

    @pl.when(has_far)
    def _():
        far_turn(half - 1, 0)

    stacked = acc[...].reshape(cols, CHUNK).astype(jnp.bfloat16)

    def route(g, carry):
        at = pl.ds(pl.multiple_of(g * (batch * lines), 16), batch * lines)
        send_part[at] = jnp.dot(pick[at], stacked, preferred_element_type=f32).astype(jnp.bfloat16)
        return carry

    lax.fori_loop(0, ndev // batch, route, 0)

    def part_copy(o, slot):
        return pltpu.make_async_remote_copy(
            src_ref=send_part.at[pl.ds(pl.multiple_of(o * lines, 16), lines)],
            dst_ref=recv_part.at[slot],
            send_sem=part_send.at[o],
            recv_sem=part_recv.at[slot],
            device_id={"src": o // nrcv, "rcv": lax.rem(o, nrcv)},
            device_id_type=MESH,
        )

    def send_one(k, carry):
        part_copy(lax.rem(me + k, ndev), me).start()
        return carry

    lax.fori_loop(1, ndev, send_one, 0)
    recv_part[me] = send_part[pl.ds(pl.multiple_of(me * lines, 16), lines)]

    def take_part(k, carry):
        o = lax.rem(me + k, ndev)
        part_copy(o, o).wait_recv()
        return carry

    lax.fori_loop(1, ndev, take_part, 0)
    for rr in range(nrcv):
        for pp in range(2):

            def add(z, total):
                return total + recv_part[(2 * z + pp) * nrcv + rr].astype(f32)

            total = lax.fori_loop(0, nsrc // 2, add, jnp.zeros((lines, CHUNK), f32))
            out_ref[rr * 2 + pp] = total / norm

    for t in range(half):
        for k in range(2 * windows):
            near_copy(t, k).wait_send()

    @pl.when(sends_far)
    def _():
        for t in range(half):
            for k in range(2 * windows):
                far_copy(t, k).wait_send()

    halo_copy.wait_send()

    @pl.when(s + 1 < nsrc)
    def _():
        lab_copy.wait_send()

    def end_count(k, carry):
        count_copy(lax.rem(s + k, nsrc), s).wait_send()
        return carry

    lax.fori_loop(1, nsrc, end_count, 0)

    def end_part(k, carry):
        part_copy(lax.rem(me + k, ndev), me).wait_send()
        return carry

    lax.fori_loop(1, ndev, end_part, 0)


def per_device(spectra, pair_bins, owners):
    local, windows, _, width = spectra.shape
    nbins = owners.shape[0]
    nsrc = lax.axis_size("src")
    nrcv = lax.axis_size("rcv")
    ndev = nsrc * nrcv
    chunks = width // CHUNK
    half = chunks // 2
    lines = CAP * 2 * half
    lanes = -(-nbins // 128) * 128
    group = 8
    x = spectra.reshape(local, windows * 2, width).transpose(1, 0, 2)
    bin_ids = jnp.arange(nbins, dtype=jnp.int32)
    same = owners[:, None] == owners[None, :]
    earlier = bin_ids[None, :] < bin_ids[:, None]
    rows = owners * CAP + jnp.sum((same & earlier).astype(jnp.int32), axis=1)
    rows_row = jnp.pad(rows, (0, lanes - nbins), constant_values=-1)[None]
    tiled = jnp.tile(rows, 2 * half)[None]
    dims = (nsrc, nrcv, nbins, local, windows, chunks, group)
    bf16, f32 = jnp.bfloat16, jnp.float32
    dma = pltpu.SemaphoreType.DMA
    vmem = pl.BlockSpec(memory_space=pltpu.VMEM)
    out = pl.pallas_call(
        functools.partial(kernel, dims),
        out_shape=jax.ShapeDtypeStruct((2 * nrcv, lines, CHUNK), f32),
        in_specs=[vmem] * 5,
        out_specs=vmem,
        scratch_shapes=[
            pltpu.VMEM((chunks, 2 * windows, local, CHUNK), bf16),
            pltpu.VMEM((half, 2 * windows, local, CHUNK), bf16),
            pltpu.VMEM((half, 2 * windows, local, CHUNK), bf16),
            pltpu.VMEM((2 * windows, local, EDGE), bf16),
            pltpu.VMEM((windows * local, width + 2 * EDGE), bf16),
            pltpu.VMEM((windows * local, width + 2 * EDGE), bf16),
            pltpu.VMEM((CHUNK + 2 * EDGE, CHUNK), bf16),
            pltpu.VMEM((2, nbins * local, local), bf16),
            pltpu.VMEM((2 * windows, local, CHUNK), f32),
            pltpu.VMEM((2 * windows, group * local, CHUNK), f32),
            pltpu.VMEM((half, 2, nbins, CHUNK), f32),
            pltpu.VMEM((ndev * lines, half * 2 * nbins), bf16),
            pltpu.VMEM((ndev * lines, CHUNK), bf16),
            pltpu.VMEM((ndev, lines, CHUNK), bf16),
            pltpu.VMEM((local, local), jnp.int32),
            pltpu.VMEM((8, lanes), f32),
            pltpu.VMEM((nsrc, 8, lanes), f32),
            dma((half, 2 * windows)),
            dma((half, 2 * windows)),
            dma((half, 2 * windows)),
            dma((half, 2 * windows)),
            dma((2,)),
            dma((2,)),
            dma((nsrc,)),
            dma((nsrc,)),
            dma((ndev,)),
            dma((ndev,)),
        ],
        compiler_params=pltpu.CompilerParams(
            collective_id=0, has_side_effects=True, vmem_limit_bytes=48 * 1024 * 1024
        ),
    )(x, pair_bins, pair_bins.T, rows_row, tiled)
    out = out.reshape(nrcv * 2, CAP, 2, half, CHUNK).transpose(1, 2, 0, 3, 4)
    return out.reshape(CAP, 2, nrcv * width)


def solution(mesh):
    in_specs = (P(("groups", "src"), None, None, "rcv"), P(("groups", "src"), None), P("groups"))
    out_specs = P(("groups", "src", "rcv"), None, None)
    return jax.shard_map(
        per_device, mesh=mesh, in_specs=in_specs, out_specs=out_specs, check_vma=False
    )
```

```python
import functools

import jax
import jax.numpy as jnp
from jax import lax
from jax.experimental import pallas as pl
from jax.experimental.pallas import tpu as pltpu
from jax.sharding import PartitionSpec as P

HALF = 32
CAP = 2
EDGE = 128
CHUNK = 256
smooth_eps = 1e-06
MESH = pl.DeviceIdType.MESH


def kernel(
    dims,
    x_ref,
    lab_ref,
    owners_ref,
    out_ref,
    white,
    near,
    far,
    halo,
    mag_hi,
    mag_lo,
    band,
    onehot,
    own,
    prod,
    acc,
    pick,
    send_part,
    recv_part,
    lab_in,
    count_out,
    count_in,
    near_send,
    near_recv,
    far_send,
    far_recv,
    halo_sems,
    lab_sems,
    count_send,
    count_recv,
    part_send,
    part_recv,
):
    nsrc, nrcv, nbins, local, windows, chunks, group = dims
    half = chunks // 2
    width = chunks * CHUNK
    ndev = nsrc * nrcv
    s = lax.axis_index("src")
    r = lax.axis_index("rcv")
    me = s * nrcv + r
    par = lax.rem(s, 2)
    f32 = jnp.float32

    barrier = pltpu.get_barrier_semaphore()

    def greet(k, carry):
        o = lax.rem(me + k, ndev)
        pl.semaphore_signal(
            barrier,
            inc=1,
            device_id={"src": o // nrcv, "rcv": lax.rem(o, nrcv)},
            device_id_type=MESH,
        )
        return carry

    lax.fori_loop(1, ndev, greet, 0)

    def place(h, t):
        return h * half + r * (half - 1) + t * (1 - 2 * r)

    def put_magnitude(re, im, row, at, size):
        re = re.astype(f32)
        im = im.astype(f32)
        m = jnp.sqrt(re * re + im * im)
        hi = m.astype(jnp.bfloat16)
        mag_hi[pl.ds(row, local), pl.ds(at, size)] = hi
        mag_lo[pl.ds(row, local), pl.ds(at, size)] = (m - hi.astype(f32)).astype(jnp.bfloat16)

    zero = jnp.zeros((windows * local, EDGE), jnp.bfloat16)
    for buffer in (mag_hi, mag_lo):
        buffer[:, :EDGE] = zero
        buffer[:, EDGE + width :] = zero

    def magnitudes(j, carry):
        at = pl.ds(pl.multiple_of(j * CHUNK, 128), CHUNK)
        for w in range(windows):
            put_magnitude(
                x_ref[2 * w, :, at],
                x_ref[2 * w + 1, :, at],
                w * local,
                pl.multiple_of(EDGE + j * CHUNK, 128),
                CHUNK,
            )
        return carry

    def inside(j):
        return jnp.minimum(jnp.maximum(j, 0), chunks - 1)

    for t in range(-1, 2):
        magnitudes(inside(place(1 - par, t)), 0)
    tall = CHUNK + 2 * EDGE
    k_ids = lax.broadcasted_iota(jnp.int32, (tall, CHUNK), 0) - EDGE
    n_ids = lax.broadcasted_iota(jnp.int32, (tall, CHUNK), 1)
    band[...] = jnp.where((k_ids >= n_ids - HALF) & (k_ids <= n_ids + HALF), 1.0, 0.0).astype(
        jnp.bfloat16
    )

    def whiten(j):
        span = pl.ds(pl.multiple_of(j * CHUNK, 128), tall)
        total = jnp.dot(mag_hi[:, span], band[...], preferred_element_type=f32)
        total = total + jnp.dot(mag_lo[:, span], band[...], preferred_element_type=f32)
        inverse = 1.0 / (total / (2 * HALF + 1) + smooth_eps)
        for w in range(windows):
            part = inverse[w * local : (w + 1) * local]
            for p in range(2):
                raw = x_ref[2 * w + p, :, pl.ds(pl.multiple_of(j * CHUNK, 128), CHUNK)]
                white[j, 2 * w + p] = (raw.astype(f32) * part).astype(jnp.bfloat16)

    partner = s + 1 - 2 * par
    beyond = s + 2 - 4 * par
    sends_far = (beyond >= 0) & (beyond < nsrc)
    back = s - 2 + 4 * par
    has_far = (back >= 0) & (back < nsrc)

    def near_copy(t, k):
        return pltpu.make_async_remote_copy(
            src_ref=white.at[place(1 - par, t), k],
            dst_ref=near.at[t, k],
            send_sem=near_send.at[t, k],
            recv_sem=near_recv.at[t, k],
            device_id={"src": partner},
            device_id_type=MESH,
        )

    def far_copy(t, k):
        return pltpu.make_async_remote_copy(
            src_ref=near.at[t, k],
            dst_ref=far.at[t, k],
            send_sem=far_send.at[t, k],
            recv_sem=far_recv.at[t, k],
            device_id={"src": beyond},
            device_id_type=MESH,
        )

    halo_copy = pltpu.make_async_remote_copy(
        src_ref=x_ref.at[
            :, :, pl.ds(pl.multiple_of((1 - r) * (width - EDGE), 128), EDGE)
        ],
        dst_ref=halo,
        send_sem=halo_sems.at[0],
        recv_sem=halo_sems.at[1],
        device_id={"rcv": 1 - r},
        device_id_type=MESH,
    )
    lab_copy = pltpu.make_async_remote_copy(
        src_ref=lab_ref,
        dst_ref=lab_in,
        send_sem=lab_sems.at[0],
        recv_sem=lab_sems.at[1],
        device_id={"src": s + 1},
        device_id_type=MESH,
    )

    whiten(place(1 - par, 0))
    pl.semaphore_wait(barrier, ndev - 1)
    halo_copy.start()

    def send_near(t):
        for k in range(2 * windows):
            near_copy(t, k).start()

    send_near(0)

    @pl.when(s + 1 < nsrc)
    def _():
        lab_copy.start()

    def send_next(t, carry):
        magnitudes(inside(place(1 - par, t + 1)), 0)
        whiten(place(1 - par, t))
        send_near(t)
        return carry

    lax.fori_loop(1, half - 1, send_next, 0)
    magnitudes(inside(place(1 - par, half)), 0)
    halo_copy.wait_recv()
    for w in range(windows):
        put_magnitude(
            halo[2 * w],
            halo[2 * w + 1],
            w * local,
            pl.multiple_of((1 - r) * (EDGE + width), 128),
            EDGE,
        )
    whiten(place(1 - par, half - 1))
    send_near(half - 1)

    labels = lab_ref[...]
    lanes = count_out.shape[1]
    lane_ids = lax.broadcasted_iota(jnp.int32, (8, lanes), 1)
    valid = (s + 1 < nsrc).astype(f32)

    def expand(b, counted):
        hits = jnp.where(labels == b, 1.0, 0.0).astype(f32)
        onehot[0, pl.ds(pl.multiple_of(b * local, 16), local), :] = hits.astype(jnp.bfloat16)
        found = jnp.sum(jnp.sum(hits, axis=0, keepdims=True), axis=1, keepdims=True)
        return counted + jnp.where(lane_ids == b, found, 0.0)

    counted = lax.fori_loop(0, nbins, expand, jnp.zeros((8, lanes), f32)) * valid
    count_out[...] = counted
    count_in[s] = counted

    def count_copy(o, slot):
        return pltpu.make_async_remote_copy(
            src_ref=count_out,
            dst_ref=count_in.at[slot],
            send_sem=count_send.at[o],
            recv_sem=count_recv.at[slot],
            device_id={"src": o},
            device_id_type=MESH,
        )

    def send_count(k, carry):
        count_copy(lax.rem(s + k, nsrc), s).start()
        return carry

    lax.fori_loop(1, nsrc, send_count, 0)

    def relay(t, k):
        near_copy(t, k).wait_recv()

        @pl.when(sends_far)
        def _():
            far_copy(t, k).start()

    relay(0, 0)

    def keep_magnitude(t, carry):
        return magnitudes(place(par, t), carry)

    lax.fori_loop(0, half, keep_magnitude, 0)

    relay(0, 1)

    def keep(t, carry):
        whiten(place(par, t))
        return carry

    lax.fori_loop(0, half, keep, 0)

    relay(0, 2)

    @pl.when(s > 0)
    def _():
        lab_copy.wait_recv()
        previous = jnp.transpose(lab_in[...].astype(f32)).astype(jnp.int32)

        def expand_previous(b, carry):
            onehot[1, pl.ds(pl.multiple_of(b * local, 16), local), :] = jnp.where(
                previous == b, 1.0, 0.0
            ).astype(jnp.bfloat16)
            return carry

        lax.fori_loop(0, nbins, expand_previous, 0)

    relay(0, 3)
    owned = owners_ref[...]
    b_rows = lax.broadcasted_iota(jnp.int32, (nbins, nbins), 0)
    b_cols = lax.broadcasted_iota(jnp.int32, (nbins, nbins), 1)
    column = jnp.sum(jnp.where(b_rows == b_cols, owned, 0).astype(f32), axis=1, keepdims=True)
    earlier = jnp.where((column.astype(jnp.int32) == owned) & (b_rows < b_cols), 1.0, 0.0)
    slots = jnp.sum(earlier.astype(f32), axis=0, keepdims=True)
    rows_row = owned.astype(f32) * CAP + slots
    spread = jnp.where(
        lax.broadcasted_iota(jnp.int32, (nbins, 2 * half * nbins), 0)
        == lax.rem(lax.broadcasted_iota(jnp.int32, (nbins, 2 * half * nbins), 1), nbins),
        1.0,
        0.0,
    ).astype(f32)
    tiled = jnp.dot(
        jnp.broadcast_to(rows_row, (8, nbins)),
        spread,
        precision=lax.Precision.HIGHEST,
        preferred_element_type=f32,
    )[0:1].astype(jnp.int32)
    rows_row = rows_row.astype(jnp.int32)
    lines = CAP * 2 * half
    cols = half * 2 * nbins
    batch = 16
    row_ids = lax.broadcasted_iota(jnp.int32, (batch * lines, cols), 0)
    col_ids = lax.broadcasted_iota(jnp.int32, (batch * lines, cols), 1)
    row_line = lax.rem(row_ids, 2 * half)
    col_turn = col_ids // (2 * nbins)
    col_line = lax.rem(col_ids // nbins, 2) * half + r * (half - 1) + col_turn * (1 - 2 * r)
    same_line = row_line == col_line
    row_slot = row_ids // (2 * half)

    def prepare(g, carry):
        chosen = same_line & (tiled == row_slot + g * (batch * CAP))
        at = pl.ds(pl.multiple_of(g * (batch * lines), 16), batch * lines)
        pick[at] = jnp.where(chosen, 1.0, 0.0).astype(jnp.bfloat16)
        return carry

    lax.fori_loop(0, ndev // batch, prepare, 0)

    def correlate(which, other, t, first):
        for k in range(2 * windows):
            own[k] = white[place(par, t), k].astype(f32)
        sign = (1 - 2 * which).astype(f32)
        rows = group * local

        def some(g, carry):
            picked = onehot[which, pl.ds(pl.multiple_of(g * rows, 16), rows), :]
            for k in range(2 * windows):
                prod[k] = jnp.dot(picked, other[t, k], preferred_element_type=f32)
            res, ims = [], []
            for b in range(group):
                at = slice(b * local, (b + 1) * local)
                re = jnp.zeros((local, CHUNK), f32)
                im = jnp.zeros((local, CHUNK), f32)
                for w in range(windows):
                    p_re, p_im = prod[2 * w, at], prod[2 * w + 1, at]
                    o_re, o_im = own[2 * w], own[2 * w + 1]
                    re = re + (o_re * p_re + o_im * p_im)
                    im = im + (o_im * p_re - o_re * p_im)
                res.append(jnp.sum(re, axis=0, keepdims=True))
                ims.append(jnp.sum(im, axis=0, keepdims=True))
            at = pl.ds(pl.multiple_of(g * group, group), group)
            re = jnp.concatenate(res, axis=0)
            im = jnp.concatenate(ims, axis=0) * sign
            if first:
                acc[t, 0, at] = re
                acc[t, 1, at] = im
            else:
                acc[t, 0, at] += re
                acc[t, 1, at] += im
            return carry

        lax.fori_loop(0, nbins // group, some, 0)

    def near_turn(t):
        correlate(par, near, t, True)

    def far_turn(t):
        for k in range(2 * windows):
            far_copy(t, k).wait_recv()
        correlate(1 - par, far, t, False)

    def turn(t, carry):
        relay(t, 0)
        near_turn(t - 1)
        for k in range(1, 2 * windows - 1):
            relay(t, k)

        @pl.when(has_far)
        def _():
            far_turn(t - 1)

        relay(t, 2 * windows - 1)
        return carry

    lax.fori_loop(1, half, turn, 0)
    near_turn(half - 1)

    def take_count(k, carry):
        o = lax.rem(s + k, nsrc)
        count_copy(o, o).wait_recv()
        return carry

    lax.fori_loop(1, nsrc, take_count, 0)
    counts = jnp.sum(count_in[...], axis=0)[0:1, :nbins]
    mine = [
        jnp.sum(jnp.where(rows_row == me * CAP + c, counts, 0.0), axis=1, keepdims=True)
        for c in range(CAP)
    ]
    line_ids = lax.broadcasted_iota(jnp.int32, (lines, 1), 0) // (2 * half)
    norm = jnp.zeros((lines, 1), f32)
    for c in range(CAP):
        norm = jnp.where(line_ids == c, jnp.sqrt(jnp.maximum(mine[c], 1.0)), norm)

    @pl.when(has_far)
    def _():
        far_turn(half - 1)

    stacked = acc[...].reshape(cols, CHUNK).astype(jnp.bfloat16)

    def route(g, carry):
        at = pl.ds(pl.multiple_of(g * (batch * lines), 16), batch * lines)
        send_part[at] = jnp.dot(pick[at], stacked, preferred_element_type=f32).astype(jnp.bfloat16)
        return carry

    lax.fori_loop(0, ndev // batch, route, 0)

    def part_copy(o, slot):
        return pltpu.make_async_remote_copy(
            src_ref=send_part.at[pl.ds(pl.multiple_of(o * lines, 16), lines)],
            dst_ref=recv_part.at[slot],
            send_sem=part_send.at[o],
            recv_sem=part_recv.at[slot],
            device_id={"src": o // nrcv, "rcv": lax.rem(o, nrcv)},
            device_id_type=MESH,
        )

    def send_one(k, carry):
        part_copy(lax.rem(me + k, ndev), me).start()
        return carry

    lax.fori_loop(1, ndev, send_one, 0)
    recv_part[me] = send_part[pl.ds(pl.multiple_of(me * lines, 16), lines)]

    def take_part(k, carry):
        o = lax.rem(me + k, ndev)
        part_copy(o, o).wait_recv()
        return carry

    lax.fori_loop(1, ndev, take_part, 0)
    for rr in range(nrcv):
        for pp in range(2):

            def add(z, total):
                return total + recv_part[(2 * z + pp) * nrcv + rr].astype(f32)

            total = lax.fori_loop(0, nsrc // 2, add, jnp.zeros((lines, CHUNK), f32))
            out_ref[rr * 2 + pp] = total / norm

    for t in range(half):
        for k in range(2 * windows):
            near_copy(t, k).wait_send()

    @pl.when(sends_far)
    def _():
        for t in range(half):
            for k in range(2 * windows):
                far_copy(t, k).wait_send()

    halo_copy.wait_send()

    @pl.when(s + 1 < nsrc)
    def _():
        lab_copy.wait_send()

    def end_count(k, carry):
        count_copy(lax.rem(s + k, nsrc), s).wait_send()
        return carry

    lax.fori_loop(1, nsrc, end_count, 0)

    def end_part(k, carry):
        part_copy(lax.rem(me + k, ndev), me).wait_send()
        return carry

    lax.fori_loop(1, ndev, end_part, 0)


def per_device(spectra, pair_bins, owners):
    local, windows, _, width = spectra.shape
    nbins = owners.shape[0]
    nsrc = lax.axis_size("src")
    nrcv = lax.axis_size("rcv")
    ndev = nsrc * nrcv
    chunks = width // CHUNK
    half = chunks // 2
    lines = CAP * 2 * half
    lanes = -(-nbins // 128) * 128
    group = 8
    x = spectra.reshape(local, windows * 2, width).transpose(1, 0, 2)
    dims = (nsrc, nrcv, nbins, local, windows, chunks, group)
    bf16, f32 = jnp.bfloat16, jnp.float32
    dma = pltpu.SemaphoreType.DMA
    vmem = pl.BlockSpec(memory_space=pltpu.VMEM)
    out = pl.pallas_call(
        functools.partial(kernel, dims),
        out_shape=jax.ShapeDtypeStruct((2 * nrcv, lines, CHUNK), f32),
        in_specs=[vmem] * 3,
        out_specs=vmem,
        scratch_shapes=[
            pltpu.VMEM((chunks, 2 * windows, local, CHUNK), bf16),
            pltpu.VMEM((half, 2 * windows, local, CHUNK), bf16),
            pltpu.VMEM((half, 2 * windows, local, CHUNK), bf16),
            pltpu.VMEM((2 * windows, local, EDGE), bf16),
            pltpu.VMEM((windows * local, width + 2 * EDGE), bf16),
            pltpu.VMEM((windows * local, width + 2 * EDGE), bf16),
            pltpu.VMEM((CHUNK + 2 * EDGE, CHUNK), bf16),
            pltpu.VMEM((2, nbins * local, local), bf16),
            pltpu.VMEM((2 * windows, local, CHUNK), f32),
            pltpu.VMEM((2 * windows, group * local, CHUNK), f32),
            pltpu.VMEM((half, 2, nbins, CHUNK), f32),
            pltpu.VMEM((ndev * lines, half * 2 * nbins), bf16),
            pltpu.VMEM((ndev * lines, CHUNK), bf16),
            pltpu.VMEM((ndev, lines, CHUNK), bf16),
            pltpu.VMEM((local, local), jnp.int32),
            pltpu.VMEM((8, lanes), f32),
            pltpu.VMEM((nsrc, 8, lanes), f32),
            dma((half, 2 * windows)),
            dma((half, 2 * windows)),
            dma((half, 2 * windows)),
            dma((half, 2 * windows)),
            dma((2,)),
            dma((2,)),
            dma((nsrc,)),
            dma((nsrc,)),
            dma((ndev,)),
            dma((ndev,)),
        ],
        compiler_params=pltpu.CompilerParams(
            collective_id=0, has_side_effects=True, vmem_limit_bytes=48 * 1024 * 1024
        ),
    )(x, pair_bins, owners[None])
    out = out.reshape(nrcv * 2, CAP, 2, half, CHUNK).transpose(1, 2, 0, 3, 4)
    return out.reshape(CAP, 2, nrcv * width)


def solution(mesh):
    in_specs = (P(("groups", "src"), None, None, "rcv"), P(("groups", "src"), None), P("groups"))
    out_specs = P(("groups", "src", "rcv"), None, None)
    return jax.shard_map(
        per_device, mesh=mesh, in_specs=in_specs, out_specs=out_specs, check_vma=False
    )
```

```python
import functools
import math

import jax
import jax.numpy as jnp
from jax import lax
from jax.experimental import pallas as pl
from jax.experimental.pallas import tpu as pltpu
from jax.sharding import PartitionSpec as P

HALF = 32
CAP = 2
EDGE = 128
CHUNK = 256
smooth_eps = 1e-06
MESH = pl.DeviceIdType.MESH


def kernel(
    dims,
    x_ref,
    lab_ref,
    owners_ref,
    out_ref,
    white,
    near,
    far,
    halo,
    mag_hi,
    mag_lo,
    band,
    onehot,
    own,
    prod,
    acc,
    pick,
    send_part,
    recv_part,
    lab_out,
    lab_in,
    count_out,
    count_in,
    near_send,
    near_recv,
    far_send,
    far_recv,
    halo_sems,
    lab_sems,
    count_send,
    count_recv,
    part_send,
    part_recv,
):
    nsrc, nrcv, nbins, local, windows, chunks, group = dims
    half = chunks // 2
    width = chunks * CHUNK
    ndev = nsrc * nrcv
    s = lax.axis_index("src")
    r = lax.axis_index("rcv")
    me = s * nrcv + r
    par = lax.rem(s, 2)
    f32 = jnp.float32

    barrier = pltpu.get_barrier_semaphore()

    def greet(k, carry):
        o = lax.rem(me + k, ndev)
        pl.semaphore_signal(
            barrier,
            inc=1,
            device_id={"src": o // nrcv, "rcv": lax.rem(o, nrcv)},
            device_id_type=MESH,
        )
        return carry

    lax.fori_loop(1, ndev, greet, 0)

    def place(h, t):
        return h * half + r * (half - 1) + t * (1 - 2 * r)

    def put_magnitude(re, im, row, at, size):
        re = re.astype(f32)
        im = im.astype(f32)
        m = jnp.sqrt(re * re + im * im)
        hi = m.astype(jnp.bfloat16)
        mag_hi[pl.ds(row, local), pl.ds(at, size)] = hi
        mag_lo[pl.ds(row, local), pl.ds(at, size)] = (m - hi.astype(f32)).astype(jnp.bfloat16)

    zero = jnp.zeros((windows * local, EDGE), jnp.bfloat16)
    for buffer in (mag_hi, mag_lo):
        buffer[:, :EDGE] = zero
        buffer[:, EDGE + width :] = zero

    def magnitudes(j, carry):
        at = pl.ds(pl.multiple_of(j * CHUNK, 128), CHUNK)
        for w in range(windows):
            put_magnitude(
                x_ref[2 * w, :, at],
                x_ref[2 * w + 1, :, at],
                w * local,
                pl.multiple_of(EDGE + j * CHUNK, 128),
                CHUNK,
            )
        return carry

    def inside(j):
        return jnp.minimum(jnp.maximum(j, 0), chunks - 1)

    for t in range(-1, 2):
        magnitudes(inside(place(1 - par, t)), 0)
    tall = CHUNK + 2 * EDGE
    k_ids = lax.broadcasted_iota(jnp.int32, (tall, CHUNK), 0) - EDGE
    n_ids = lax.broadcasted_iota(jnp.int32, (tall, CHUNK), 1)
    band[...] = jnp.where((k_ids >= n_ids - HALF) & (k_ids <= n_ids + HALF), 1.0, 0.0).astype(
        jnp.bfloat16
    )

    def whiten(j):
        span = pl.ds(pl.multiple_of(j * CHUNK, 128), tall)
        total = jnp.dot(mag_hi[:, span], band[...], preferred_element_type=f32)
        total = total + jnp.dot(mag_lo[:, span], band[...], preferred_element_type=f32)
        inverse = 1.0 / (total / (2 * HALF + 1) + smooth_eps)
        for w in range(windows):
            part = inverse[w * local : (w + 1) * local]
            for p in range(2):
                raw = x_ref[2 * w + p, :, pl.ds(pl.multiple_of(j * CHUNK, 128), CHUNK)]
                white[j, 2 * w + p] = (raw.astype(f32) * part).astype(jnp.bfloat16)

    partner = s + 1 - 2 * par
    beyond = s + 2 - 4 * par
    sends_far = (beyond >= 0) & (beyond < nsrc)
    back = s - 2 + 4 * par
    has_far = (back >= 0) & (back < nsrc)

    def near_copy(t, k):
        return pltpu.make_async_remote_copy(
            src_ref=white.at[place(1 - par, t), k],
            dst_ref=near.at[t, k],
            send_sem=near_send.at[t, k],
            recv_sem=near_recv.at[t, k],
            device_id={"src": partner},
            device_id_type=MESH,
        )

    def far_copy(t, k):
        return pltpu.make_async_remote_copy(
            src_ref=near.at[t, k],
            dst_ref=far.at[t, k],
            send_sem=far_send.at[t, k],
            recv_sem=far_recv.at[t, k],
            device_id={"src": beyond},
            device_id_type=MESH,
        )

    halo_copy = pltpu.make_async_remote_copy(
        src_ref=x_ref.at[
            :, :, pl.ds(pl.multiple_of((1 - r) * (width - EDGE), 128), EDGE)
        ],
        dst_ref=halo,
        send_sem=halo_sems.at[0],
        recv_sem=halo_sems.at[1],
        device_id={"rcv": 1 - r},
        device_id_type=MESH,
    )
    lab_copy = pltpu.make_async_remote_copy(
        src_ref=lab_out,
        dst_ref=lab_in,
        send_sem=lab_sems.at[0],
        recv_sem=lab_sems.at[1],
        device_id={"src": s + 1},
        device_id_type=MESH,
    )

    lab_out[...] = lab_ref[...].astype(f32).astype(jnp.bfloat16)
    whiten(place(1 - par, 0))
    pl.semaphore_wait(barrier, ndev - 1)
    halo_copy.start()

    def send_near(t):
        for k in range(2 * windows):
            near_copy(t, k).start()

    send_near(0)

    @pl.when(s + 1 < nsrc)
    def _():
        lab_copy.start()

    def send_next(t, carry):
        magnitudes(inside(place(1 - par, t + 1)), 0)
        whiten(place(1 - par, t))
        send_near(t)
        return carry

    lax.fori_loop(1, half - 1, send_next, 0)
    magnitudes(inside(place(1 - par, half)), 0)
    halo_copy.wait_recv()
    for w in range(windows):
        put_magnitude(
            halo[2 * w],
            halo[2 * w + 1],
            w * local,
            pl.multiple_of((1 - r) * (EDGE + width), 128),
            EDGE,
        )
    whiten(place(1 - par, half - 1))
    send_near(half - 1)

    labels = lab_ref[...]
    lanes = count_out.shape[1]
    lane_ids = lax.broadcasted_iota(jnp.int32, (1, lanes), 1)
    valid = (s + 1 < nsrc).astype(f32)

    def expand(b, counted):
        hits = jnp.where(labels == b, 1.0, 0.0).astype(f32)
        onehot[0, pl.ds(pl.multiple_of(b * local, 16), local), :] = hits.astype(jnp.bfloat16)
        found = jnp.sum(jnp.sum(hits, axis=0, keepdims=True), axis=1, keepdims=True)
        return counted + jnp.where(lane_ids == b, found, 0.0)

    counted = lax.fori_loop(0, nbins, expand, jnp.zeros((1, lanes), f32)) * valid
    count_out[...] = counted
    count_in[s] = counted

    def count_copy(o, slot):
        return pltpu.make_async_remote_copy(
            src_ref=count_out,
            dst_ref=count_in.at[slot],
            send_sem=count_send.at[o],
            recv_sem=count_recv.at[slot],
            device_id={"src": o},
            device_id_type=MESH,
        )

    def send_count(k, carry):
        count_copy(lax.rem(s + k, nsrc), s).start()
        return carry

    lax.fori_loop(1, nsrc, send_count, 0)

    def relay(t, k):
        near_copy(t, k).wait_recv()

        @pl.when(sends_far)
        def _():
            far_copy(t, k).start()

    relay(0, 0)

    def keep_magnitude(t, carry):
        return magnitudes(place(par, t), carry)

    lax.fori_loop(0, half, keep_magnitude, 0)

    relay(0, 1)

    def keep(t, carry):
        whiten(place(par, t))
        return carry

    lax.fori_loop(0, half, keep, 0)

    relay(0, 2)

    @pl.when(s > 0)
    def _():
        lab_copy.wait_recv()
        previous = jnp.transpose(lab_in[...].astype(f32)).astype(jnp.int32)

        def expand_previous(b, carry):
            onehot[1, pl.ds(pl.multiple_of(b * local, 16), local), :] = jnp.where(
                previous == b, 1.0, 0.0
            ).astype(jnp.bfloat16)
            return carry

        lax.fori_loop(0, nbins, expand_previous, 0)

    relay(0, 3)
    owned = owners_ref[...]
    b_rows = lax.broadcasted_iota(jnp.int32, (nbins, nbins), 0)
    b_cols = lax.broadcasted_iota(jnp.int32, (nbins, nbins), 1)
    column = jnp.sum(jnp.where(b_rows == b_cols, owned, 0).astype(f32), axis=1, keepdims=True)
    earlier = jnp.where((column.astype(jnp.int32) == owned) & (b_rows < b_cols), 1.0, 0.0)
    slots = jnp.sum(earlier.astype(f32), axis=0, keepdims=True)
    rows_row = owned.astype(f32) * CAP + slots
    spread = jnp.where(
        lax.broadcasted_iota(jnp.int32, (nbins, 2 * half * nbins), 0)
        == lax.rem(lax.broadcasted_iota(jnp.int32, (nbins, 2 * half * nbins), 1), nbins),
        1.0,
        0.0,
    ).astype(f32)
    tiled = jnp.dot(
        jnp.broadcast_to(rows_row, (8, nbins)),
        spread,
        precision=lax.Precision.HIGHEST,
        preferred_element_type=f32,
    )[0:1].astype(jnp.int32)
    rows_row = rows_row.astype(jnp.int32)
    lines = CAP * 2 * half
    cols = half * 2 * nbins
    batch = 16
    row_ids = lax.broadcasted_iota(jnp.int32, (batch * lines, cols), 0)
    col_ids = lax.broadcasted_iota(jnp.int32, (batch * lines, cols), 1)
    row_line = lax.rem(row_ids, 2 * half)
    col_turn = col_ids // (2 * nbins)
    col_line = lax.rem(col_ids // nbins, 2) * half + r * (half - 1) + col_turn * (1 - 2 * r)
    same_line = row_line == col_line
    row_slot = row_ids // (2 * half)

    def prepare(g, carry):
        chosen = same_line & (tiled == row_slot + g * (batch * CAP))
        at = pl.ds(pl.multiple_of(g * (batch * lines), 16), batch * lines)
        pick[at] = jnp.where(chosen, 1.0, 0.0).astype(jnp.bfloat16)
        return carry

    lax.fori_loop(0, ndev // batch, prepare, 0)

    def correlate(which, other, t, first):
        for k in range(2 * windows):
            own[k] = white[place(par, t), k].astype(f32)
        sign = (1 - 2 * which).astype(f32)
        rows = group * local

        def some(g, carry):
            picked = onehot[which, pl.ds(pl.multiple_of(g * rows, 16), rows), :]
            for k in range(2 * windows):
                prod[k] = jnp.dot(picked, other[t, k], preferred_element_type=f32)
            res, ims = [], []
            for b in range(group):
                at = slice(b * local, (b + 1) * local)
                re = jnp.zeros((local, CHUNK), f32)
                im = jnp.zeros((local, CHUNK), f32)
                for w in range(windows):
                    p_re, p_im = prod[2 * w, at], prod[2 * w + 1, at]
                    o_re, o_im = own[2 * w], own[2 * w + 1]
                    re = re + (o_re * p_re + o_im * p_im)
                    im = im + (o_im * p_re - o_re * p_im)
                res.append(jnp.sum(re, axis=0, keepdims=True))
                ims.append(jnp.sum(im, axis=0, keepdims=True))
            at = pl.ds(pl.multiple_of(g * group, group), group)
            re = jnp.concatenate(res, axis=0)
            im = jnp.concatenate(ims, axis=0) * sign
            if first:
                acc[t, 0, at] = re
                acc[t, 1, at] = im
            else:
                acc[t, 0, at] += re
                acc[t, 1, at] += im
            return carry

        lax.fori_loop(0, nbins // group, some, 0)

    def near_turn(t):
        correlate(par, near, t, True)

    def far_turn(t):
        for k in range(2 * windows):
            far_copy(t, k).wait_recv()
        correlate(1 - par, far, t, False)

    def turn(t, carry):
        relay(t, 0)
        near_turn(t - 1)
        for k in range(1, 2 * windows - 1):
            relay(t, k)

        @pl.when(has_far)
        def _():
            far_turn(t - 1)

        relay(t, 2 * windows - 1)
        return carry

    lax.fori_loop(1, half, turn, 0)
    near_turn(half - 1)

    def take_count(k, carry):
        o = lax.rem(s + k, nsrc)
        count_copy(o, o).wait_recv()
        return carry

    lax.fori_loop(1, nsrc, take_count, 0)
    counts = jnp.sum(count_in[...], axis=0)[0:1, :nbins]
    mine = [
        jnp.sum(jnp.where(rows_row == me * CAP + c, counts, 0.0), axis=1, keepdims=True)
        for c in range(CAP)
    ]
    line_ids = lax.broadcasted_iota(jnp.int32, (lines, 1), 0) // (2 * half)
    norm = jnp.zeros((lines, 1), f32)
    for c in range(CAP):
        norm = jnp.where(line_ids == c, jnp.sqrt(jnp.maximum(mine[c], 1.0)), norm)

    @pl.when(has_far)
    def _():
        far_turn(half - 1)

    stacked = acc[...].reshape(cols, CHUNK).astype(jnp.bfloat16)

    def route(g, carry):
        at = pl.ds(pl.multiple_of(g * (batch * lines), 16), batch * lines)
        send_part[at] = jnp.dot(pick[at], stacked, preferred_element_type=f32).astype(jnp.bfloat16)
        return carry

    lax.fori_loop(0, ndev // batch, route, 0)

    def part_copy(o, slot):
        return pltpu.make_async_remote_copy(
            src_ref=send_part.at[pl.ds(pl.multiple_of(o * lines, 16), lines)],
            dst_ref=recv_part.at[slot],
            send_sem=part_send.at[o],
            recv_sem=part_recv.at[slot],
            device_id={"src": o // nrcv, "rcv": lax.rem(o, nrcv)},
            device_id_type=MESH,
        )

    def send_one(k, carry):
        part_copy(lax.rem(me + k, ndev), me).start()
        return carry

    lax.fori_loop(1, ndev, send_one, 0)
    recv_part[me] = send_part[pl.ds(pl.multiple_of(me * lines, 16), lines)]

    def take_part(k, carry):
        o = lax.rem(me + k, ndev)
        part_copy(o, o).wait_recv()
        return carry

    lax.fori_loop(1, ndev, take_part, 0)
    for rr in range(nrcv):
        for pp in range(2):

            def add(z, total):
                return total + recv_part[(2 * z + pp) * nrcv + rr].astype(f32)

            total = lax.fori_loop(0, nsrc // 2, add, jnp.zeros((lines, CHUNK), f32))
            out_ref[rr * 2 + pp] = total / norm

    for t in range(half):
        for k in range(2 * windows):
            near_copy(t, k).wait_send()

    @pl.when(sends_far)
    def _():
        for t in range(half):
            for k in range(2 * windows):
                far_copy(t, k).wait_send()

    halo_copy.wait_send()

    @pl.when(s + 1 < nsrc)
    def _():
        lab_copy.wait_send()

    def end_count(k, carry):
        count_copy(lax.rem(s + k, nsrc), s).wait_send()
        return carry

    lax.fori_loop(1, nsrc, end_count, 0)

    def end_part(k, carry):
        part_copy(lax.rem(me + k, ndev), me).wait_send()
        return carry

    lax.fori_loop(1, ndev, end_part, 0)


def per_device(spectra, pair_bins, owners):
    local, windows, _, width = spectra.shape
    nbins = owners.shape[0]
    nsrc = lax.axis_size("src")
    nrcv = lax.axis_size("rcv")
    ndev = nsrc * nrcv
    chunks = width // CHUNK
    half = chunks // 2
    lines = CAP * 2 * half
    lanes = -(-nbins // 128) * 128
    group = math.gcd(nbins, 16)
    x = spectra.reshape(local, windows * 2, width).transpose(1, 0, 2)
    dims = (nsrc, nrcv, nbins, local, windows, chunks, group)
    bf16, f32 = jnp.bfloat16, jnp.float32
    dma = pltpu.SemaphoreType.DMA
    vmem = pl.BlockSpec(memory_space=pltpu.VMEM)
    out = pl.pallas_call(
        functools.partial(kernel, dims),
        out_shape=jax.ShapeDtypeStruct((2 * nrcv, lines, CHUNK), f32),
        in_specs=[vmem] * 3,
        out_specs=vmem,
        scratch_shapes=[
            pltpu.VMEM((chunks, 2 * windows, local, CHUNK), bf16),
            pltpu.VMEM((half, 2 * windows, local, CHUNK), bf16),
            pltpu.VMEM((half, 2 * windows, local, CHUNK), bf16),
            pltpu.VMEM((2 * windows, local, EDGE), bf16),
            pltpu.VMEM((windows * local, width + 2 * EDGE), bf16),
            pltpu.VMEM((windows * local, width + 2 * EDGE), bf16),
            pltpu.VMEM((CHUNK + 2 * EDGE, CHUNK), bf16),
            pltpu.VMEM((2, nbins * local, local), bf16),
            pltpu.VMEM((2 * windows, local, CHUNK), f32),
            pltpu.VMEM((2 * windows, group * local, CHUNK), f32),
            pltpu.VMEM((half, 2, nbins, CHUNK), f32),
            pltpu.VMEM((ndev * lines, half * 2 * nbins), bf16),
            pltpu.VMEM((ndev * lines, CHUNK), bf16),
            pltpu.VMEM((ndev, lines, CHUNK), bf16),
            pltpu.VMEM((local, local), bf16),
            pltpu.VMEM((local, local), bf16),
            pltpu.VMEM((1, lanes), f32),
            pltpu.VMEM((nsrc, 1, lanes), f32),
            dma((half, 2 * windows)),
            dma((half, 2 * windows)),
            dma((half, 2 * windows)),
            dma((half, 2 * windows)),
            dma((2,)),
            dma((2,)),
            dma((nsrc,)),
            dma((nsrc,)),
            dma((ndev,)),
            dma((ndev,)),
        ],
        compiler_params=pltpu.CompilerParams(
            collective_id=0, has_side_effects=True, vmem_limit_bytes=48 * 1024 * 1024
        ),
    )(x, pair_bins, owners[None])
    out = out.reshape(nrcv * 2, CAP, 2, half, CHUNK).transpose(1, 2, 0, 3, 4)
    return out.reshape(CAP, 2, nrcv * width)


def solution(mesh):
    in_specs = (P(("groups", "src"), None, None, "rcv"), P(("groups", "src"), None), P("groups"))
    out_specs = P(("groups", "src", "rcv"), None, None)
    return jax.shard_map(
        per_device, mesh=mesh, in_specs=in_specs, out_specs=out_specs, check_vma=False
    )
```
